768 devices in a mesh: row: 192 (over y, z, core), col: 4 (over x).
Axes of the slice: x: 4, y: 8, z: 12, core: 2. Of those that a mesh axis runs over, the one named last changes fastest.
Arguments:
- matrix: bfloat16 [49152, 24576], P('row', 'col'), may hold values from 7 to 180000
- left_t: float32 [32, 49152], P(None, 'row'), may hold values from 0.5 to 2
- right: float32 [32, 24576], P(None, 'col'), may hold values from 0.5 to 2
Outputs:
- new_left_t: float32 [32, 49152], P(None, 'row')
- new_right: float32 [32, 24576], P(None, 'col')
The draws below stay inside these ranges and needn't reach their ends.
All inputs are finite; a program needn't handle non-finite values.
Results may differ from the reference program's by a relative error of at most 0.0003.
Values sent between devices are 32-bit elements; how exact they have to be, the bound alone decides.
No kernel may reach another device: no remote copies, remote signals or barrier semaphores. Data moves between devices by JAX's collectives and lax.ppermute only.
A program may use at most 32 MiB of HBM per device.

```python
import math
import jax
import jax.numpy as jnp
from jax import lax

RANK = 32
ROW_DEV = 256
COL_DEV = 6144
ROWS = 49152
COLS = 24576


def draw_matrix(key, part):
    key_rows = jax.random.fold_in(key, 11)
    key_cols = jax.random.fold_in(key, 12)
    key_cells = jax.random.fold_in(key, 13)
    key_pair = jax.random.fold_in(key, 14)
    row_blocks = ROWS // ROW_DEV
    slice_width = COL_DEV // row_blocks
    row_scale = jnp.exp(jax.random.uniform(key_rows, (row_blocks,), jnp.float32, 0.0, math.log(10.0)))
    col_scale = jnp.exp(jax.random.uniform(key_cols, (COLS // COL_DEV,), jnp.float32, 0.0, math.log(3.0)))
    noise = jnp.clip(0.5 * jax.random.normal(key_cells, (ROWS, COLS), jnp.float32), -1.5, 1.5)
    offset = jax.random.randint(key_pair, (), 0, row_blocks)
    row_block_of = jnp.arange(ROWS, dtype=jnp.int32) // ROW_DEV
    slice_of = jnp.arange(COLS, dtype=jnp.int32) % COL_DEV // slice_width
    paired = slice_of[None, :] == (row_block_of[:, None] + offset) % row_blocks
    heavy = jnp.where(paired, 40.0, 1.0).astype(jnp.float32)
    rows_full = jnp.repeat(row_scale, ROW_DEV)
    cols_full = jnp.repeat(col_scale, COL_DEV)
    values = 32.0 * rows_full[:, None] * cols_full[None, :] * jnp.exp(noise) * heavy
    return values.astype(jnp.bfloat16)


def block_levels(own_key, shape, shards, smallest, high):
    factor_of = 1.0
    for dim, parts in shards:
        heights = jax.random.uniform(jax.random.fold_in(jax.random.fold_in(own_key, 6), dim), (parts,), jnp.float32, smallest / len(shards), high / len(shards))
        factor_of = factor_of * jnp.repeat(jnp.exp(heights), shape[dim] // parts).reshape((-1,) + (1,) * (len(shape) - 1 - dim))
    return factor_of


def setup_inputs(seed: int = 0) -> dict:
    key_list = jax.random.split(jax.random.key(seed), 4)
    matrix = draw_matrix(jax.random.fold_in(key_list[3], 71), 0)
    left_t = jnp.clip(jnp.exp(math.log(2.0) - 1.3862944 * jax.random.uniform(key_list[1], (RANK, ROWS), jnp.float32) ** block_levels(key_list[1], (RANK, ROWS), ((1, 192),), -0.2, 0.2)), 0.5, 2.0)
    right = jnp.clip(jnp.exp(math.log(2.0) - 1.3862944 * jax.random.uniform(key_list[2], (RANK, COLS), jnp.float32) ** block_levels(key_list[2], (RANK, COLS), ((1, 4),), -0.2, 0.2)), 0.5, 2.0)
    return dict(matrix=matrix, left_t=left_t, right=right)


HIGH = lax.Precision.HIGHEST


def reference(matrix, left_t, right):
    right_mass = jnp.sum(right, axis=1)
    blocks = ROWS // ROW_DEV

    def left_block(block_index):
        first_row = (block_index * ROW_DEV).astype(jnp.int32)
        tile_values = lax.dynamic_slice_in_dim(matrix, first_row, ROW_DEV, 0).astype(jnp.float32)
        left_block_t = lax.dynamic_slice_in_dim(left_t, first_row, ROW_DEV, 1)
        product = lax.dot_general(left_block_t, right, (((0,), (0,)), ((), ())), precision=HIGH, preferred_element_type=jnp.float32)
        quotient = tile_values / product
        numerator = lax.dot_general(right, quotient, (((1,), (1,)), ((), ())), precision=HIGH, preferred_element_type=jnp.float32)
        return left_block_t * numerator / right_mass[:, None]

    stacked = lax.map(left_block, jnp.arange(blocks, dtype=jnp.int32))
    new_left_t = jnp.transpose(stacked, (1, 0, 2)).reshape(RANK, ROWS)
    left_mass = jnp.sum(new_left_t, axis=1)

    def right_block(accumulated, block_index):
        first_row = (block_index * ROW_DEV).astype(jnp.int32)
        tile_values = lax.dynamic_slice_in_dim(matrix, first_row, ROW_DEV, 0).astype(jnp.float32)
        left_block_t = lax.dynamic_slice_in_dim(new_left_t, first_row, ROW_DEV, 1)
        product = lax.dot_general(left_block_t, right, (((0,), (0,)), ((), ())), precision=HIGH, preferred_element_type=jnp.float32)
        quotient = tile_values / product
        accumulated = accumulated + jnp.dot(left_block_t, quotient, precision=HIGH, preferred_element_type=jnp.float32)
        return accumulated, None

    totals, _ = lax.scan(right_block, jnp.zeros((RANK, COLS), jnp.float32), jnp.arange(blocks, dtype=jnp.int32))
    new_right = right * totals / left_mass[:, None]
    return new_left_t, new_right
```

```python
import jax
import jax.numpy as jnp
from jax import lax
from jax.sharding import Mesh, PartitionSpec as P

HIGH = lax.Precision.HIGHEST
PLANE = ("y", "z")
SUB, LANE = 8, 128


def local(matrix, left_t, right):
    rank, rows = left_t.shape
    cols = right.shape[1]
    n_col = lax.axis_size("x")
    n_plane = lax.axis_size(PLANE)
    core = lax.axis_index("c")
    pair = [(0, 1), (1, 0)]
    tile_values = matrix.astype(jnp.float32)

    product = lax.dot_general(
        left_t, right, (((0,), (0,)), ((), ())), precision=HIGH, preferred_element_type=jnp.float32
    )
    quotient = tile_values / product
    part = lax.dot_general(
        right, quotient, (((1,), (1,)), ((), ())), precision=HIGH, preferred_element_type=jnp.float32
    )
    mass_part = jnp.broadcast_to(jnp.sum(right, axis=1)[:, None], (rank, LANE))
    sent = jnp.concatenate([part, mass_part], axis=1)
    sent = jnp.broadcast_to(sent[None], (n_col, *sent.shape))
    got = jnp.sum(lax.all_to_all(sent, "x", 0, 0), axis=0)
    new_left_t = left_t * got[:, :rows] / got[:, rows : rows + 1]

    product_two = lax.dot_general(
        new_left_t, right, (((0,), (0,)), ((), ())), precision=HIGH, preferred_element_type=jnp.float32
    )
    quotient_two = tile_values / product_two
    totals = jnp.dot(new_left_t, quotient_two, precision=HIGH, preferred_element_type=jnp.float32)
    mass = jnp.sum(new_left_t, axis=1)

    bands, strips = rank // SUB, cols // LANE
    n_tiles = bands * strips
    half = n_tiles // 2
    each = half // n_plane
    tiles = totals.reshape(bands, SUB, strips, LANE).transpose(0, 2, 1, 3).reshape(n_tiles, SUB, LANE)
    mass_tiles = jnp.broadcast_to(mass.reshape(bands, SUB)[:, :, None], (bands, SUB, LANE))
    own = lax.dynamic_slice_in_dim(tiles, core * half, half, 0)
    other = lax.dynamic_slice_in_dim(tiles, (1 - core) * half, half, 0)
    own_mass = lax.dynamic_slice_in_dim(mass_tiles, core * bands // 2, bands // 2, 0)
    other_mass = lax.dynamic_slice_in_dim(mass_tiles, (1 - core) * bands // 2, bands // 2, 0)
    there = lax.ppermute(jnp.concatenate([other, other_mass], axis=0), "c", pair)
    summed = own + there[:half]
    summed_mass = own_mass + there[half:]
    per_band = n_plane // (bands // 2)
    mass_of = jnp.repeat(summed_mass, per_band, axis=0)
    message = jnp.concatenate([summed.reshape(n_plane, each * SUB, LANE), mass_of], axis=1)
    arrived = jnp.sum(lax.all_to_all(message, PLANE, 0, 0), axis=0)
    done = arrived[: each * SUB].reshape(each, SUB, LANE) / arrived[None, each * SUB :]
    spread = jnp.broadcast_to(done[None], (n_plane, each, SUB, LANE))
    mine = lax.all_to_all(spread, PLANE, 0, 0).reshape(half, SUB, LANE)
    theirs = lax.ppermute(mine, "c", pair)
    low = jnp.where(core == 0, mine, theirs)
    high = jnp.where(core == 0, theirs, mine)
    whole = jnp.concatenate([low, high], axis=0)
    whole = whole.reshape(bands, strips, SUB, LANE).transpose(0, 2, 1, 3).reshape(rank, cols)
    return new_left_t, right * whole


def factor(mesh):
    n_row, n_col = mesh.shape["row"], mesh.shape["col"]
    n_z = 12 if n_row % 24 == 0 else 2
    shape = (n_row // (2 * n_z), n_z, 2, n_col)
    return Mesh(mesh.devices.reshape(shape), ("y", "z", "c", "x"))


def solution(mesh):
    row = ("y", "z", "c")
    return jax.shard_map(
        local,
        mesh=factor(mesh),
        in_specs=(P(row, "x"), P(None, row), P(None, "x")),
        out_specs=(P(None, row), P(None, "x")),
        check_vma=False,
    )
```

```python
import functools

import jax
import jax.numpy as jnp
from jax import lax
from jax.experimental import pallas as pl
from jax.experimental.pallas import tpu as pltpu
from jax.sharding import Mesh, PartitionSpec as P

SUB, LANE = 8, 128
F32, BF16 = jnp.float32, jnp.bfloat16
NT = (((1,), (1,)), ((), ()))


def split(x):
    high = x.astype(BF16)
    return high, (x - high.astype(F32)).astype(BF16)


def dot(a, b):
    return jnp.dot(a, b, preferred_element_type=F32)


def stack_left(left):
    rank = left.shape[0]
    wide = jnp.concatenate([left] * 4, axis=0).T
    high = wide.astype(BF16).astype(F32)
    lane = lax.broadcasted_iota(jnp.int32, wide.shape, 1)
    return jnp.where(lane < 2 * rank, high, wide - high).astype(BF16)


def pack_column(column):
    bands = column.shape[0] // SUB
    lane = lax.broadcasted_iota(jnp.int32, (SUB, LANE), 1) // (LANE // bands)
    tile = jnp.zeros((SUB, LANE), F32)
    for b in range(bands):
        tile = jnp.where(lane == b, column[b * SUB : (b + 1) * SUB], tile)
    return tile


def unpack_column(tile, bands):
    lane = lax.broadcasted_iota(jnp.int32, (SUB, LANE), 1) // (LANE // bands)
    return [jnp.max(jnp.where(lane == b, tile, 0.0), axis=1, keepdims=True) for b in range(bands)]


def left_kernel(matrix_ref, left_ref, right_ref, out_ref, stacked, total, mass):
    step = pl.program_id(0)
    rank, rows = left_ref.shape

    @pl.when(step == 0)
    def _():
        stacked[...] = stack_left(left_ref[...])
        total[...] = jnp.zeros_like(total)
        mass[...] = jnp.zeros_like(mass)

    right = right_ref[...]
    high, low = split(right)
    product = dot(stacked[...], jnp.concatenate([high, low, high, low], axis=0))
    quotient = matrix_ref[...].astype(F32) / product
    q_high, q_low = split(quotient)
    both = lax.dot_general(
        jnp.concatenate([high, low], axis=0), q_high, NT, preferred_element_type=F32
    )
    rest = lax.dot_general(high, q_low, NT, preferred_element_type=F32)
    total[...] += both[:rank] + both[rank:] + rest
    mass[...] += sum(right[:, s : s + LANE] for s in range(0, right.shape[1], LANE))

    @pl.when(step == pl.num_programs(0) - 1)
    def _():
        bands, strips = rank // SUB, rows // LANE
        packed = pack_column(jnp.sum(mass[...], axis=1, keepdims=True))
        for peer in range(out_ref.shape[0]):
            for b in range(bands):
                for s in range(strips):
                    out_ref[peer, b * strips + s] = total[
                        b * SUB : (b + 1) * SUB, s * LANE : (s + 1) * LANE
                    ]
            out_ref[peer, bands * strips] = packed


def right_kernel(first, half_ref, matrix_ref, source_ref, left_ref, right_ref, *refs):
    del half_ref
    if first:
        out_ref, new_ref, stacked, pair = refs
    else:
        out_ref, stacked, pair = refs
    step = pl.program_id(0)
    rank, rows = left_ref.shape
    bands, strips = rank // SUB, rows // LANE
    n_out = out_ref.shape[0]

    @pl.when(step == 0)
    def _():
        if first:
            got = sum(source_ref[peer] for peer in range(source_ref.shape[0]))
            masses = unpack_column(got[bands * strips], bands)
            for b in range(bands):
                for s in range(strips):
                    at = (slice(b * SUB, (b + 1) * SUB), slice(s * LANE, (s + 1) * LANE))
                    new_ref[at] = left_ref[at] * got[b * strips + s] / masses[b]
            new = new_ref[...]
        else:
            new = left_ref[...]
        stacked[...] = stack_left(new)
        high, low = split(new)
        pair[...] = jnp.concatenate([high, low], axis=0)
        out_ref[n_out - 1] = pack_column(jnp.sum(new, axis=1, keepdims=True))

    high, low = split(right_ref[...])
    product = dot(stacked[...], jnp.concatenate([high, low, high, low], axis=0))
    quotient = matrix_ref[...].astype(F32) / product
    q_high, q_low = split(quotient)
    both = dot(pair[...], q_high)
    rest = dot(pair[:rank], q_low)
    total = both[:rank] + both[rank:] + rest
    wide = total.shape[1] // LANE
    per_band = (n_out - 1) // bands
    for b in range(bands):
        for s in range(wide):
            out_ref[b * per_band + step * wide + s] = total[
                b * SUB : (b + 1) * SUB, s * LANE : (s + 1) * LANE
            ]


def block_of(width):
    return 1024 if width % 1024 == 0 else LANE


def cost(rows, cols, rank):
    return pl.CostEstimate(
        flops=14 * rows * cols * rank, bytes_accessed=2 * rows * cols + 8 * rank * cols, transcendentals=rows * cols
    )


def left_phase(matrix, left_t, right, n_col):
    (rank, rows), cols = left_t.shape, right.shape[1]
    width = block_of(cols)
    n_tiles = rank * rows // (SUB * LANE) + 1
    return pl.pallas_call(
        left_kernel,
        name="left_phase",
        out_shape=jax.ShapeDtypeStruct((n_col, n_tiles, SUB, LANE), F32),
        grid=(cols // width,),
        in_specs=[
            pl.BlockSpec((rows, width), lambda i: (0, i)),
            pl.BlockSpec((rank, rows), lambda i: (0, 0)),
            pl.BlockSpec((rank, width), lambda i: (0, i)),
        ],
        out_specs=pl.BlockSpec((n_col, n_tiles, SUB, LANE), lambda i: (0, 0, 0, 0)),
        scratch_shapes=[
            pltpu.VMEM((rows, 4 * rank), BF16),
            pltpu.VMEM((rank, rows), F32),
            pltpu.VMEM((rank, LANE), F32),
        ],
        cost_estimate=cost(rows, cols, rank),
    )(matrix, left_t, right)


def right_phase(first, half, matrix, source, left_t, right):
    (rank, rows), cols = left_t.shape, right.shape[1] // 2
    width = block_of(cols)
    steps = cols // width
    n_tiles = rank * cols // (SUB * LANE) + 1
    whole = lambda shape: pl.BlockSpec(shape, lambda i, h: (0,) * len(shape))
    out_shape = [jax.ShapeDtypeStruct((n_tiles, SUB, LANE), F32)]
    out_specs = [whole((n_tiles, SUB, LANE))]
    if first:
        out_shape.append(jax.ShapeDtypeStruct((rank, rows), F32))
        out_specs.append(whole((rank, rows)))
    return pl.pallas_call(
        functools.partial(right_kernel, first),
        name="right_first" if first else "right_second",
        out_shape=out_shape,
        grid_spec=pltpu.PrefetchScalarGridSpec(
            num_scalar_prefetch=1,
            grid=(steps,),
            in_specs=[
                pl.BlockSpec((rows, width), lambda i, h: (0, h[0] * steps + i)),
                whole(source.shape),
                whole((rank, rows)),
                pl.BlockSpec((rank, width), lambda i, h: (0, h[0] * steps + i)),
            ],
            out_specs=out_specs,
            scratch_shapes=[pltpu.VMEM((rows, 4 * rank), BF16), pltpu.VMEM((2 * rank, rows), BF16)],
        ),
        cost_estimate=cost(rows, cols, rank),
    )(half, matrix, source, left_t, right)


def local(matrix, left_t, right):
    rank, cols = right.shape
    n_y, n_z, n_col = lax.axis_size("y"), lax.axis_size("z"), lax.axis_size("x")
    core = lax.axis_index("c")
    partner = [(0, 1), (1, 0)]

    sent = left_phase(matrix, left_t, right, n_col)
    got = lax.all_to_all(sent, "x", 0, 0)
    other = jnp.reshape(1 - core, (1,)).astype(jnp.int32)
    own = jnp.reshape(core, (1,)).astype(jnp.int32)
    for_partner, new_left_t = right_phase(True, other, matrix, got, left_t, right)
    there = lax.ppermute(for_partner, "c", partner)
    (here,) = right_phase(False, own, matrix, new_left_t, new_left_t, right)

    bands, strips = rank // SUB, cols // (2 * LANE)
    half = bands * strips
    summed = here + there
    masses = jnp.broadcast_to(summed[half:][None], (n_y, 1, SUB, LANE))
    message = jnp.concatenate([summed[:half].reshape(n_y, n_z, SUB, LANE), masses], axis=1)
    line = jnp.sum(lax.all_to_all(message, "y", 0, 0), axis=0)
    masses = jnp.broadcast_to(line[n_z:], (n_z, SUB, LANE))
    point = jnp.sum(lax.all_to_all(jnp.stack([line[:n_z], masses], axis=1), "z", 0, 0), axis=0)
    band = (lax.axis_index("y") * n_z + lax.axis_index("z")) // strips
    mass = lax.dynamic_slice(point[1], (0, band * (LANE // bands)), (SUB, 1))
    done = point[0] / mass
    line = lax.all_to_all(jnp.broadcast_to(done[None], (n_z, SUB, LANE)), "z", 0, 0)
    mine = lax.all_to_all(jnp.broadcast_to(line[None], (n_y, n_z, SUB, LANE)), "y", 0, 0)
    mine = mine.reshape(bands, strips, SUB, LANE)
    theirs = lax.ppermute(mine, "c", partner)
    low = jnp.where(core == 0, mine, theirs)
    high = jnp.where(core == 0, theirs, mine)
    whole = jnp.concatenate([low, high], axis=1).transpose(0, 2, 1, 3).reshape(rank, cols)
    return new_left_t, right * whole


def factor(mesh):
    n_row, n_col = mesh.shape["row"], mesh.shape["col"]
    n_z = 12 if n_row % 24 == 0 else 2
    shape = (n_row // (2 * n_z), n_z, 2, n_col)
    return Mesh(mesh.devices.reshape(shape), ("y", "z", "c", "x"))


def solution(mesh):
    row = ("y", "z", "c")
    return jax.shard_map(
        local,
        mesh=factor(mesh),
        in_specs=(P(row, "x"), P(None, row), P(None, "x")),
        out_specs=(P(None, row), P(None, "x")),
        check_vma=False,
    )
```

```python
import functools

import jax
import jax.numpy as jnp
from jax import lax
from jax.experimental import pallas as pl
from jax.experimental.pallas import tpu as pltpu
from jax.sharding import Mesh, PartitionSpec as P

SUB, LANE = 8, 128
F32, BF16 = jnp.float32, jnp.bfloat16
NT = (((1,), (1,)), ((), ()))


def split(x):
    high = x.astype(BF16)
    return high, (x - high.astype(F32)).astype(BF16)


def dot(a, b):
    return jnp.dot(a, b, preferred_element_type=F32)


def stack_left(left):
    rank = left.shape[0]
    wide = jnp.concatenate([left] * 4, axis=0).T
    high = wide.astype(BF16).astype(F32)
    lane = lax.broadcasted_iota(jnp.int32, wide.shape, 1)
    return jnp.where(lane < 2 * rank, high, wide - high).astype(BF16)


def pack_column(column):
    bands = column.shape[0] // SUB
    lane = lax.broadcasted_iota(jnp.int32, (SUB, LANE), 1) // (LANE // bands)
    tile = jnp.zeros((SUB, LANE), F32)
    for b in range(bands):
        tile = jnp.where(lane == b, column[b * SUB : (b + 1) * SUB], tile)
    return tile


def unpack_column(tile, bands):
    lane = lax.broadcasted_iota(jnp.int32, (SUB, LANE), 1) // (LANE // bands)
    return [jnp.max(jnp.where(lane == b, tile, 0.0), axis=1, keepdims=True) for b in range(bands)]


def quotient_of(stacked, right, cells):
    high, low = split(right)
    product = dot(stacked, jnp.concatenate([high, low, high, low], axis=0))
    return high, low, split(cells.astype(F32) / product)


def left_kernel(matrix_ref, left_ref, right_ref, out_ref):
    rank, rows = left_ref.shape
    cols = right_ref.shape[1]
    width, chunk = widths(cols)
    stacked = stack_left(left_ref[...])

    def body(i, carry):
        added, summed = carry
        for c in range(width // chunk):
            at = pl.ds(pl.multiple_of(i * width + c * chunk, chunk), chunk)
            right = right_ref[:, at]
            high, low, (q_high, q_low) = quotient_of(stacked, right, matrix_ref[:, at])
            both = lax.dot_general(
                jnp.concatenate([high, low], axis=0), q_high, NT, preferred_element_type=F32
            )
            rest = lax.dot_general(high, q_low, NT, preferred_element_type=F32)
            added += both[:rank] + both[rank:] + rest
            summed += sum(right[:, s : s + LANE] for s in range(0, chunk, LANE))
        return added, summed

    total, mass = lax.fori_loop(
        0, cols // width, body, (jnp.zeros((rank, rows), F32), jnp.zeros((rank, LANE), F32))
    )
    bands, strips = rank // SUB, rows // LANE
    packed = pack_column(jnp.sum(mass, axis=1, keepdims=True))
    for peer in range(out_ref.shape[0]):
        for b in range(bands):
            for s in range(strips):
                out_ref[peer, b * strips + s] = total[b * SUB : (b + 1) * SUB, s * LANE : (s + 1) * LANE]
        out_ref[peer, bands * strips] = packed


def right_kernel(first, half_ref, matrix_ref, left_ref, right_ref, *refs):
    rank, rows = left_ref.shape
    bands, strips = rank // SUB, rows // LANE
    if first:
        source_ref, out_ref, kept_ref, new_ref = refs
        got = sum(source_ref[peer] for peer in range(source_ref.shape[0]))
        masses = unpack_column(got[bands * strips], bands)
        for b in range(bands):
            for s in range(strips):
                at = (slice(b * SUB, (b + 1) * SUB), slice(s * LANE, (s + 1) * LANE))
                value = left_ref[at] * got[b * strips + s] / masses[b]
                new_ref[at] = value
                kept_ref[at] = value
        new = kept_ref[...]
    else:
        (out_ref,) = refs
        new = left_ref[...]
    stacked = stack_left(new)
    new_high, new_low = split(new)
    pair = jnp.concatenate([new_high, new_low], axis=0)

    half = right_ref.shape[1] // 2
    width, chunk = widths(half)
    per_band = half // LANE
    wide = chunk // LANE
    sums = jnp.sum(new, axis=1, keepdims=True)
    for b in range(bands):
        out_ref[bands * per_band + b] = jnp.broadcast_to(sums[b * SUB : (b + 1) * SUB], (SUB, LANE))
    start = half_ref[0] * half

    def body(i, carry):
        for c in range(width // chunk):
            at = pl.ds(pl.multiple_of(start + i * width + c * chunk, chunk), chunk)
            _, _, (q_high, q_low) = quotient_of(stacked, right_ref[:, at], matrix_ref[:, at])
            both = dot(pair, q_high)
            total = both[:rank] + both[rank:] + dot(new_high, q_low)
            for b in range(bands):
                for s in range(wide):
                    out_ref[b * per_band + i * (width // LANE) + c * wide + s] = total[
                        b * SUB : (b + 1) * SUB, s * LANE : (s + 1) * LANE
                    ]
        return carry

    lax.fori_loop(0, half // width, body, 0)


def widths(cols):
    width = 1024 if cols % 1024 == 0 else LANE
    return width, min(width, 256)


def cost(rows, cols, rank):
    return pl.CostEstimate(
        flops=14 * rows * cols * rank, bytes_accessed=2 * rows * cols + 8 * rank * cols, transcendentals=rows * cols
    )


ON_CHIP = pl.BlockSpec(memory_space=pltpu.VMEM)
PARAMS = pltpu.CompilerParams(vmem_limit_bytes=32 << 20)


def left_phase(matrix, left_t, right, n_col):
    (rank, rows), cols = left_t.shape, right.shape[1]
    n_tiles = rank * rows // (SUB * LANE) + 1
    return pl.pallas_call(
        left_kernel,
        name="left_phase",
        out_shape=jax.ShapeDtypeStruct((n_col, n_tiles, SUB, LANE), F32),
        in_specs=[ON_CHIP] * 3,
        out_specs=ON_CHIP,
        compiler_params=PARAMS,
        cost_estimate=cost(rows, cols, rank),
    )(matrix, left_t, right)


def right_phase(half, matrix, left_t, right, *source):
    (rank, rows), cols = left_t.shape, right.shape[1] // 2
    n_tiles = rank * cols // (SUB * LANE) + rank // SUB
    out_shape = [jax.ShapeDtypeStruct((n_tiles, SUB, LANE), F32)]
    if source:
        out_shape += [jax.ShapeDtypeStruct((rank, rows), F32)] * 2
    return pl.pallas_call(
        functools.partial(right_kernel, bool(source)),
        name="right_first" if source else "right_second",
        out_shape=out_shape,
        in_specs=[pl.BlockSpec(memory_space=pltpu.SMEM)] + [ON_CHIP] * (3 + len(source)),
        out_specs=[ON_CHIP] * len(out_shape),
        compiler_params=PARAMS,
        cost_estimate=cost(rows, cols, rank),
    )(half, matrix, left_t, right, *source)


def local(matrix, left_t, right):
    rank, cols = right.shape
    n_col, n_group = lax.axis_size("x"), lax.axis_size(("y", "zl"))
    n_far = lax.axis_size("zh")
    core = lax.axis_index("c")
    partner = [(0, 1), (1, 0)]
    own = jnp.reshape(core, (1,)).astype(jnp.int32)
    other = 1 - own
    left_t, own, other = lax.optimization_barrier((left_t, own, other))

    got = lax.all_to_all(left_phase(matrix, left_t, right, n_col), "x", 0, 0)
    for_partner, kept, new_left_t = right_phase(other, matrix, left_t, right, got)
    there = lax.ppermute(for_partner, "c", partner)
    (here,) = right_phase(own, matrix, kept, right)

    bands, strips = rank // SUB, cols // (2 * LANE)
    half = bands * strips
    each = half // n_group
    summed = here + there
    masses = jnp.repeat(summed[half:], n_group // bands, axis=0)[:, None]
    message = jnp.concatenate([summed[:half].reshape(n_group, each, SUB, LANE), masses], axis=1)
    part = jnp.sum(lax.all_to_all(message, ("y", "zl"), 0, 0), axis=0)
    part = jnp.broadcast_to(part[None], (n_far, each + 1, SUB, LANE))
    part = jnp.sum(lax.all_to_all(part, "zh", 0, 0), axis=0)
    done = part[:each] / part[each:]
    done = jnp.broadcast_to(done[None], (n_group, each, SUB, LANE))
    mine = lax.all_to_all(done, ("y", "zl"), 0, 0).reshape(bands, strips, SUB, LANE)
    theirs = lax.ppermute(mine, "c", partner)
    is_first = own[0] == 0
    low = jnp.where(is_first, mine, theirs)
    high = jnp.where(is_first, theirs, mine)
    whole = jnp.concatenate([low, high], axis=1).transpose(0, 2, 1, 3).reshape(rank, cols)
    return new_left_t, right * whole


def factor(mesh):
    n_row, n_col = mesh.shape["row"], mesh.shape["col"]
    n_far, n_near = (3, 4) if n_row % 24 == 0 else (1, 2)
    shape = (n_row // (2 * n_far * n_near), n_far, n_near, 2, n_col)
    return Mesh(mesh.devices.reshape(shape), ("y", "zh", "zl", "c", "x"))


def solution(mesh):
    row = ("y", "zh", "zl", "c")
    return jax.shard_map(
        local,
        mesh=factor(mesh),
        in_specs=(P(row, "x"), P(None, row), P(None, "x")),
        out_specs=(P(None, row), P(None, "x")),
        check_vma=False,
    )
```

```python
import functools

import jax
import jax.numpy as jnp
from jax import lax
from jax.experimental import pallas as pl
from jax.experimental.pallas import tpu as pltpu
from jax.sharding import Mesh, PartitionSpec as P

SUB, LANE = 8, 128
ROWS_OF = 2
F32, BF16 = jnp.float32, jnp.bfloat16
NT = (((1,), (1,)), ((), ()))


def split(x):
    high = x.astype(BF16)
    return high, (x - high.astype(F32)).astype(BF16)


def dot(a, b):
    return jnp.dot(a, b, preferred_element_type=F32)


def stack_left(left):
    rank = left.shape[0]
    wide = jnp.concatenate([left] * 4, axis=0).T
    high = wide.astype(BF16).astype(F32)
    lane = lax.broadcasted_iota(jnp.int32, wide.shape, 1)
    return jnp.where(lane < 2 * rank, high, wide - high).astype(BF16)


def pack_column(column):
    bands = column.shape[0] // SUB
    lane = lax.broadcasted_iota(jnp.int32, (SUB, LANE), 1) // (LANE // bands)
    tile = jnp.zeros((SUB, LANE), F32)
    for b in range(bands):
        tile = jnp.where(lane == b, column[b * SUB : (b + 1) * SUB], tile)
    return tile


def unpack_column(tile, bands):
    lane = lax.broadcasted_iota(jnp.int32, (SUB, LANE), 1) // (LANE // bands)
    return [jnp.max(jnp.where(lane == b, tile, 0.0), axis=1, keepdims=True) for b in range(bands)]


def quotient_of(stacked, right, cells):
    high, low = split(right)
    product = dot(stacked, jnp.concatenate([high, low, high, low], axis=0))
    return high, low, split(cells.astype(F32) / product)


def left_kernel(matrix_hbm, left_ref, right_ref, out_ref, matrix_ref, both_ref, rest_ref, sems):
    rank, rows = left_ref.shape
    cols = right_ref.shape[1]
    width, chunk = widths(cols)
    steps = cols // width

    def fetch(i):
        at = pl.ds(pl.multiple_of(i * width, width), width)
        return pltpu.make_async_copy(matrix_hbm.at[:, at], matrix_ref.at[:, at], sems.at[i])

    for i in range(steps):
        fetch(i).start()
    both_ref[...] = jnp.zeros_like(both_ref)
    rest_ref[...] = jnp.zeros_like(rest_ref)
    stacked = stack_left(left_ref[...])

    def body(i, summed):
        fetch(i).wait()
        highs, lows, q_highs, q_lows = [], [], [], []
        for c in range(width // chunk):
            at = pl.ds(pl.multiple_of(i * width + c * chunk, chunk), chunk)
            right = right_ref[:, at]
            high, low, (q_high, q_low) = quotient_of(stacked, right, matrix_ref[:, at])
            highs.append(high)
            lows.append(low)
            q_highs.append(q_high)
            q_lows.append(q_low)
            summed += sum(right[:, s : s + LANE] for s in range(0, chunk, LANE))
        high = jnp.concatenate(highs, axis=1)
        low = jnp.concatenate(lows, axis=1)
        both_ref[...] += lax.dot_general(
            jnp.concatenate(q_highs, axis=1), jnp.concatenate([high, low], axis=0), NT, preferred_element_type=F32
        )
        rest_ref[...] += lax.dot_general(
            jnp.concatenate(q_lows, axis=1), high, NT, preferred_element_type=F32
        )
        return summed

    mass = lax.fori_loop(0, steps, body, jnp.zeros((rank, LANE), F32))
    both = both_ref[...].T
    total = both[:rank] + both[rank:] + rest_ref[...].T
    bands, strips = rank // SUB, rows // LANE
    packed = pack_column(jnp.sum(mass, axis=1, keepdims=True))
    for peer in range(out_ref.shape[0]):
        for b in range(bands):
            for s in range(strips):
                out_ref[peer, b * strips + s] = total[b * SUB : (b + 1) * SUB, s * LANE : (s + 1) * LANE]
        out_ref[peer, bands * strips] = packed


def right_kernel(first, half_ref, matrix_ref, left_ref, right_ref, *refs):
    rank, rows = left_ref.shape
    bands, strips = rank // SUB, rows // LANE
    if first:
        source_ref, out_ref, kept_ref, new_ref = refs
        got = sum(source_ref[peer] for peer in range(source_ref.shape[0]))
        masses = unpack_column(got[bands * strips], bands)
        for b in range(bands):
            for s in range(strips):
                at = (slice(b * SUB, (b + 1) * SUB), slice(s * LANE, (s + 1) * LANE))
                value = left_ref[at] * got[b * strips + s] / masses[b]
                new_ref[at] = value
                kept_ref[at] = value
        new = kept_ref[...]
    else:
        (out_ref,) = refs
        new = left_ref[...]
    stacked = stack_left(new)
    new_high, new_low = split(new)
    pair = jnp.concatenate([new_high, new_low], axis=0)

    half = right_ref.shape[1] // 2
    width, chunk = widths(half)
    per_band = half // LANE
    wide = chunk // LANE
    sums = jnp.sum(new, axis=1, keepdims=True)
    for b in range(bands):
        out_ref[bands * per_band + b] = jnp.broadcast_to(sums[b * SUB : (b + 1) * SUB], (SUB, LANE))
    start = half_ref[0] * half

    def body(i, carry):
        for c in range(width // chunk):
            at = pl.ds(pl.multiple_of(start + i * width + c * chunk, chunk), chunk)
            _, _, (q_high, q_low) = quotient_of(stacked, right_ref[:, at], matrix_ref[:, at])
            both = dot(pair, q_high)
            total = both[:rank] + both[rank:] + dot(new_high, q_low)
            for b in range(bands):
                for s in range(wide):
                    out_ref[b * per_band + i * (width // LANE) + c * wide + s] = total[
                        b * SUB : (b + 1) * SUB, s * LANE : (s + 1) * LANE
                    ]
        return carry

    lax.fori_loop(0, half // width, body, 0)


def message_kernel(here_ref, there_ref, out_ref):
    peers, pairs = out_ref.shape[0], out_ref.shape[1] - 1
    per_tile = SUB // ROWS_OF
    each = pairs // per_tile
    half = peers * each
    bands = here_ref.shape[0] - half
    group = lax.broadcasted_iota(jnp.int32, (ROWS_OF, LANE), 1) // (LANE // per_tile)
    for b in range(bands):
        mass = here_ref[half + b] + there_ref[half + b]
        packed = jnp.zeros((ROWS_OF, LANE), F32)
        for r in range(per_tile):
            packed = jnp.where(group == r, mass[r * ROWS_OF : (r + 1) * ROWS_OF], packed)
        for p in range(b * peers // bands, (b + 1) * peers // bands):
            out_ref[p, pairs] = packed
    for t in range(half):
        tile = here_ref[t] + there_ref[t]
        for r in range(per_tile):
            out_ref[t // each, t % each * per_tile + r] = tile[r * ROWS_OF : (r + 1) * ROWS_OF]


def finish_kernel(part_ref, out_ref):
    per_tile = SUB // ROWS_OF
    pairs = part_ref.shape[1] - 1
    group = lax.broadcasted_iota(jnp.int32, (ROWS_OF, LANE), 1) // (LANE // per_tile)
    rows = [sum(part_ref[f, i] for f in range(part_ref.shape[0])) for i in range(pairs + 1)]
    mass = jnp.concatenate(
        [jnp.max(jnp.where(group == r, rows[pairs], 0.0), axis=1, keepdims=True) for r in range(per_tile)], axis=0
    )
    for e in range(out_ref.shape[1]):
        tile = jnp.concatenate(rows[e * per_tile : (e + 1) * per_tile], axis=0) / mass
        for p in range(out_ref.shape[0]):
            out_ref[p, e] = tile


def on_chip(kernel, name, shape, *args):
    return pl.pallas_call(
        kernel,
        name=name,
        out_shape=jax.ShapeDtypeStruct(shape, F32),
        in_specs=[ON_CHIP] * len(args),
        out_specs=ON_CHIP,
        compiler_params=PARAMS,
    )(*args)


def widths(cols):
    width = 1024 if cols % 1024 == 0 else LANE
    return width, min(width, 256)


def cost(rows, cols, rank):
    return pl.CostEstimate(
        flops=14 * rows * cols * rank, bytes_accessed=2 * rows * cols + 8 * rank * cols, transcendentals=rows * cols
    )


LEFT_LIMIT = 51_000_000
ON_CHIP = pl.BlockSpec(memory_space=pltpu.VMEM)
PARAMS = pltpu.CompilerParams(vmem_limit_bytes=32 << 20)


def left_phase(matrix, left_t, right, n_col):
    (rank, rows), cols = left_t.shape, right.shape[1]
    steps = cols // widths(cols)[0]
    n_tiles = rank * rows // (SUB * LANE) + 1
    return pl.pallas_call(
        left_kernel,
        name="left_phase",
        out_shape=[
            jax.ShapeDtypeStruct((n_col, n_tiles, SUB, LANE), F32),
            jax.ShapeDtypeStruct(matrix.shape, matrix.dtype),
        ],
        in_specs=[pl.BlockSpec(memory_space=pltpu.HBM), ON_CHIP, ON_CHIP],
        out_specs=[ON_CHIP] * 2,
        scratch_shapes=[
            pltpu.VMEM((rows, 2 * rank), F32),
            pltpu.VMEM((rows, rank), F32),
            pltpu.SemaphoreType.DMA((steps,)),
        ],
        compiler_params=pltpu.CompilerParams(vmem_limit_bytes=LEFT_LIMIT),
        cost_estimate=cost(rows, cols, rank),
    )(matrix, left_t, right)


def right_phase(half, matrix, left_t, right, *source):
    (rank, rows), cols = left_t.shape, right.shape[1] // 2
    n_tiles = rank * cols // (SUB * LANE) + rank // SUB
    out_shape = [jax.ShapeDtypeStruct((n_tiles, SUB, LANE), F32)]
    if source:
        out_shape += [jax.ShapeDtypeStruct((rank, rows), F32)] * 2
    return pl.pallas_call(
        functools.partial(right_kernel, bool(source)),
        name="right_first" if source else "right_second",
        out_shape=out_shape,
        in_specs=[pl.BlockSpec(memory_space=pltpu.SMEM)] + [ON_CHIP] * (3 + len(source)),
        out_specs=[ON_CHIP] * len(out_shape),
        compiler_params=PARAMS,
        cost_estimate=cost(rows, cols, rank),
    )(half, matrix, left_t, right, *source)


def local(matrix, left_t, right):
    rank, cols = right.shape
    n_col, n_group = lax.axis_size("x"), lax.axis_size(("y", "zl"))
    n_far = lax.axis_size("zh")
    core = lax.axis_index("c")
    partner = [(0, 1), (1, 0)]
    own = jnp.reshape(core, (1,)).astype(jnp.int32)
    other = 1 - own
    left_t, own, other = lax.optimization_barrier((left_t, own, other))

    sent, matrix = left_phase(matrix, left_t, right, n_col)
    got = lax.all_to_all(sent, "x", 0, 0)
    for_partner, kept, new_left_t = right_phase(other, matrix, left_t, right, got)
    there = lax.ppermute(for_partner, "c", partner)
    (here,) = right_phase(own, matrix, kept, right)

    bands, strips = rank // SUB, cols // (2 * LANE)
    half = bands * strips
    each = half // n_group
    pairs = each * (SUB // ROWS_OF)
    message = on_chip(message_kernel, "message", (n_group, pairs + 1, ROWS_OF, LANE), here, there)
    part = jnp.sum(lax.all_to_all(message, ("y", "zl"), 0, 0), axis=0)
    part = lax.all_to_all(jnp.broadcast_to(part[None], (n_far, *part.shape)), "zh", 0, 0)
    done = on_chip(finish_kernel, "finish", (n_group, each, SUB, LANE), part)
    mine = lax.all_to_all(done, ("y", "zl"), 0, 0).reshape(bands, strips, SUB, LANE)
    theirs = lax.ppermute(mine, "c", partner)
    is_first = own[0] == 0
    low = jnp.where(is_first, mine, theirs)
    high = jnp.where(is_first, theirs, mine)
    whole = jnp.concatenate([low, high], axis=1).transpose(0, 2, 1, 3).reshape(rank, cols)
    return new_left_t, right * whole


def factor(mesh):
    n_row, n_col = mesh.shape["row"], mesh.shape["col"]
    n_far, n_near = (3, 4) if n_row % 24 == 0 else (1, 2)
    shape = (n_row // (2 * n_far * n_near), n_far, n_near, 2, n_col)
    return Mesh(mesh.devices.reshape(shape), ("y", "zh", "zl", "c", "x"))


def solution(mesh):
    row = ("y", "zh", "zl", "c")
    return jax.shard_map(
        local,
        mesh=factor(mesh),
        in_specs=(P(row, "x"), P(None, row), P(None, "x")),
        out_specs=(P(None, row), P(None, "x")),
        check_vma=False,
    )
```

```python
import functools

import jax
import jax.numpy as jnp
from jax import lax
from jax.experimental import pallas as pl
from jax.experimental.pallas import tpu as pltpu
from jax.sharding import Mesh, PartitionSpec as P

SUB, LANE = 8, 128
ROWS_OF = 2
F32, BF16 = jnp.float32, jnp.bfloat16
NT = (((1,), (1,)), ((), ()))


def split(x):
    high = x.astype(BF16)
    return high, (x - high.astype(F32)).astype(BF16)


def dot(a, b):
    return jnp.dot(a, b, preferred_element_type=F32)


def stack_left(left):
    rank = left.shape[0]
    wide = jnp.concatenate([left] * 4, axis=0).T
    high = wide.astype(BF16).astype(F32)
    lane = lax.broadcasted_iota(jnp.int32, wide.shape, 1)
    return jnp.where(lane < 2 * rank, high, wide - high).astype(BF16)


def pack_column(column):
    bands = column.shape[0] // SUB
    lane = lax.broadcasted_iota(jnp.int32, (SUB, LANE), 1) // (LANE // bands)
    tile = jnp.zeros((SUB, LANE), F32)
    for b in range(bands):
        tile = jnp.where(lane == b, column[b * SUB : (b + 1) * SUB], tile)
    return tile


def unpack_column(tile, bands):
    lane = lax.broadcasted_iota(jnp.int32, (SUB, LANE), 1) // (LANE // bands)
    return [jnp.max(jnp.where(lane == b, tile, 0.0), axis=1, keepdims=True) for b in range(bands)]


def quotient_of(stacked, right, cells):
    high, low = split(right)
    product = dot(stacked, jnp.concatenate([high, low, high, low], axis=0))
    return high, low, split(cells.astype(F32) / product)


def left_kernel(matrix_hbm, left_hbm, right_hbm, out_ref, matrix_ref, left_ref, right_ref, both_ref, rest_ref, sems, left_sem):
    rank, rows = left_ref.shape
    cols = right_ref.shape[1]
    width, chunk = widths(cols)
    steps = cols // width

    def fetches(i):
        at = pl.ds(pl.multiple_of(i * width, width), width)
        return (
            pltpu.make_async_copy(right_hbm.at[:, at], right_ref.at[:, at], sems.at[0, i]),
            pltpu.make_async_copy(matrix_hbm.at[:, at], matrix_ref.at[:, at], sems.at[1, i]),
        )

    fetch_left = pltpu.make_async_copy(left_hbm, left_ref, left_sem)
    fetch_left.start()
    for i in range(steps):
        for fetch in fetches(i):
            fetch.start()
    both_ref[...] = jnp.zeros_like(both_ref)
    rest_ref[...] = jnp.zeros_like(rest_ref)
    fetch_left.wait()
    stacked = stack_left(left_ref[...])

    def body(i, summed):
        for fetch in fetches(i):
            fetch.wait()
        highs, lows, q_highs, q_lows = [], [], [], []
        for c in range(width // chunk):
            at = pl.ds(pl.multiple_of(i * width + c * chunk, chunk), chunk)
            right = right_ref[:, at]
            high, low, (q_high, q_low) = quotient_of(stacked, right, matrix_ref[:, at])
            highs.append(high)
            lows.append(low)
            q_highs.append(q_high)
            q_lows.append(q_low)
            summed += sum(right[:, s : s + LANE] for s in range(0, chunk, LANE))
        high = jnp.concatenate(highs, axis=1)
        low = jnp.concatenate(lows, axis=1)
        both_ref[...] += lax.dot_general(
            jnp.concatenate(q_highs, axis=1), jnp.concatenate([high, low], axis=0), NT, preferred_element_type=F32
        )
        rest_ref[...] += lax.dot_general(
            jnp.concatenate(q_lows, axis=1), high, NT, preferred_element_type=F32
        )
        return summed

    mass = lax.fori_loop(0, steps, body, jnp.zeros((rank, LANE), F32))
    both = both_ref[...].T
    total = both[:rank] + both[rank:] + rest_ref[...].T
    bands, strips = rank // SUB, rows // LANE
    packed = pack_column(jnp.sum(mass, axis=1, keepdims=True))
    for peer in range(out_ref.shape[0]):
        for b in range(bands):
            for s in range(strips):
                out_ref[peer, b * strips + s] = total[b * SUB : (b + 1) * SUB, s * LANE : (s + 1) * LANE]
        out_ref[peer, bands * strips] = packed


def right_kernel(first, half_ref, matrix_ref, left_ref, right_ref, *refs):
    rank, rows = left_ref.shape
    bands, strips = rank // SUB, rows // LANE
    if first:
        source_ref, out_ref, kept_ref, new_ref = refs
        got = sum(source_ref[peer] for peer in range(source_ref.shape[0]))
        masses = unpack_column(got[bands * strips], bands)
        for b in range(bands):
            for s in range(strips):
                at = (slice(b * SUB, (b + 1) * SUB), slice(s * LANE, (s + 1) * LANE))
                value = left_ref[at] * got[b * strips + s] / masses[b]
                new_ref[at] = value
                kept_ref[at] = value
        new = kept_ref[...]
    else:
        (out_ref,) = refs
        new = left_ref[...]
    stacked = stack_left(new)
    new_high, new_low = split(new)
    pair = jnp.concatenate([new_high, new_low], axis=0)

    half = right_ref.shape[1] // 2
    width, chunk = widths(half)
    per_band = half // LANE
    wide = chunk // LANE
    sums = jnp.sum(new, axis=1, keepdims=True)
    for b in range(bands):
        out_ref[bands * per_band + b] = jnp.broadcast_to(sums[b * SUB : (b + 1) * SUB], (SUB, LANE))
    start = half_ref[0] * half

    def body(i, carry):
        for c in range(width // chunk):
            at = pl.ds(pl.multiple_of(start + i * width + c * chunk, chunk), chunk)
            _, _, (q_high, q_low) = quotient_of(stacked, right_ref[:, at], matrix_ref[:, at])
            both = dot(pair, q_high)
            total = both[:rank] + both[rank:] + dot(new_high, q_low)
            for b in range(bands):
                for s in range(wide):
                    out_ref[b * per_band + i * (width // LANE) + c * wide + s] = total[
                        b * SUB : (b + 1) * SUB, s * LANE : (s + 1) * LANE
                    ]
        return carry

    lax.fori_loop(0, half // width, body, 0)


def message_kernel(here_ref, there_ref, out_ref):
    peers, pairs = out_ref.shape[0], out_ref.shape[1] - 1
    per_tile = SUB // ROWS_OF
    each = pairs // per_tile
    half = peers * each
    bands = here_ref.shape[0] - half
    group = lax.broadcasted_iota(jnp.int32, (ROWS_OF, LANE), 1) // (LANE // per_tile)
    for b in range(bands):
        mass = here_ref[half + b] + there_ref[half + b]
        packed = jnp.zeros((ROWS_OF, LANE), F32)
        for r in range(per_tile):
            packed = jnp.where(group == r, mass[r * ROWS_OF : (r + 1) * ROWS_OF], packed)
        for p in range(b * peers // bands, (b + 1) * peers // bands):
            out_ref[p, pairs] = packed
    for t in range(half):
        tile = here_ref[t] + there_ref[t]
        for r in range(per_tile):
            out_ref[t // each, t % each * per_tile + r] = tile[r * ROWS_OF : (r + 1) * ROWS_OF]


def finish_kernel(place_ref, *refs):
    *parts, out_ref = refs
    n = len(parts)
    far_of = [lax.rem(place_ref[0] - source + n, n) for source in range(n)]

    def ordered(i):
        total = None
        for far in far_of:
            value = parts[0][i]
            for d in range(1, n):
                value = jnp.where(far == d, parts[d][i], value)
            total = value if total is None else total + value
        return total

    per_tile = SUB // ROWS_OF
    pairs = parts[0].shape[0] - 1
    group = lax.broadcasted_iota(jnp.int32, (ROWS_OF, LANE), 1) // (LANE // per_tile)
    rows = [ordered(i) for i in range(pairs + 1)]
    mass = jnp.concatenate(
        [jnp.max(jnp.where(group == r, rows[pairs], 0.0), axis=1, keepdims=True) for r in range(per_tile)], axis=0
    )
    for e in range(out_ref.shape[1]):
        tile = jnp.concatenate(rows[e * per_tile : (e + 1) * per_tile], axis=0) / mass
        for p in range(out_ref.shape[0]):
            out_ref[p, e] = tile


def on_chip(kernel, name, shape, *args, scalar=None):
    scalars = () if scalar is None else (scalar,)
    return pl.pallas_call(
        kernel,
        name=name,
        out_shape=jax.ShapeDtypeStruct(shape, F32),
        in_specs=[pl.BlockSpec(memory_space=pltpu.SMEM)] * len(scalars) + [ON_CHIP] * len(args),
        out_specs=ON_CHIP,
        compiler_params=PARAMS,
    )(*scalars, *args)


def widths(cols):
    width = 1024 if cols % 1024 == 0 else LANE
    return width, min(width, 256)


def cost(rows, cols, rank):
    return pl.CostEstimate(
        flops=14 * rows * cols * rank, bytes_accessed=2 * rows * cols + 8 * rank * cols, transcendentals=rows * cols
    )


LEFT_LIMIT = 32 << 20
ON_CHIP = pl.BlockSpec(memory_space=pltpu.VMEM)
PARAMS = pltpu.CompilerParams(vmem_limit_bytes=32 << 20)


def left_phase(matrix, left_t, right, n_col):
    (rank, rows), cols = left_t.shape, right.shape[1]
    steps = cols // widths(cols)[0]
    n_tiles = rank * rows // (SUB * LANE) + 1
    return pl.pallas_call(
        left_kernel,
        name="left_phase",
        out_shape=[
            jax.ShapeDtypeStruct((n_col, n_tiles, SUB, LANE), F32),
            jax.ShapeDtypeStruct(matrix.shape, matrix.dtype),
            jax.ShapeDtypeStruct(left_t.shape, F32),
            jax.ShapeDtypeStruct(right.shape, F32),
        ],
        in_specs=[pl.BlockSpec(memory_space=pltpu.HBM)] * 3,
        out_specs=[ON_CHIP] * 4,
        scratch_shapes=[
            pltpu.VMEM((rows, 2 * rank), F32),
            pltpu.VMEM((rows, rank), F32),
            pltpu.SemaphoreType.DMA((2, steps)),
            pltpu.SemaphoreType.DMA,
        ],
        compiler_params=pltpu.CompilerParams(vmem_limit_bytes=LEFT_LIMIT),
        cost_estimate=cost(rows, cols, rank),
    )(*(pltpu.with_memory_space_constraint(a, pltpu.HBM) for a in (matrix, left_t, right)))


def right_phase(half, matrix, left_t, right, *source):
    (rank, rows), cols = left_t.shape, right.shape[1] // 2
    n_tiles = rank * cols // (SUB * LANE) + rank // SUB
    out_shape = [jax.ShapeDtypeStruct((n_tiles, SUB, LANE), F32)]
    if source:
        out_shape += [jax.ShapeDtypeStruct((rank, rows), F32)] * 2
    return pl.pallas_call(
        functools.partial(right_kernel, bool(source)),
        name="right_first" if source else "right_second",
        out_shape=out_shape,
        in_specs=[pl.BlockSpec(memory_space=pltpu.SMEM)] + [ON_CHIP] * (3 + len(source)),
        out_specs=[ON_CHIP] * len(out_shape),
        compiler_params=PARAMS,
        cost_estimate=cost(rows, cols, rank),
    )(half, matrix, left_t, right, *source)


def local(matrix, left_t, right):
    rank, cols = right.shape
    n_col, n_group = lax.axis_size("x"), lax.axis_size(("y", "zl"))
    n_far = lax.axis_size("zh")
    core = lax.axis_index("c")
    partner = [(0, 1), (1, 0)]
    own = jnp.reshape(core, (1,)).astype(jnp.int32)
    other = 1 - own
    place = jnp.reshape(lax.axis_index("zh"), (1,)).astype(jnp.int32)
    left_t, own, other, place = lax.optimization_barrier((left_t, own, other, place))

    sent, matrix, left_t, right = left_phase(matrix, left_t, right, n_col)
    got = lax.all_to_all(sent, "x", 0, 0)
    for_partner, kept, new_left_t = right_phase(other, matrix, left_t, right, got)
    there = lax.ppermute(for_partner, "c", partner)
    (here,) = right_phase(own, matrix, kept, right)

    bands, strips = rank // SUB, cols // (2 * LANE)
    half = bands * strips
    each = half // n_group
    pairs = each * (SUB // ROWS_OF)
    message = on_chip(message_kernel, "message", (n_group, pairs + 1, ROWS_OF, LANE), here, there)
    part = jnp.sum(lax.all_to_all(message, ("y", "zl"), 0, 0), axis=0)
    far = [
        lax.ppermute(part, "zh", [(i, (i + d) % n_far) for i in range(n_far)]) for d in range(1, n_far)
    ]
    done = on_chip(finish_kernel, "finish", (n_group, each, SUB, LANE), part, *far, scalar=place)
    mine = lax.all_to_all(done, ("y", "zl"), 0, 0).reshape(bands, strips, SUB, LANE)
    theirs = lax.ppermute(mine, "c", partner)
    is_first = own[0] == 0
    low = jnp.where(is_first, mine, theirs)
    high = jnp.where(is_first, theirs, mine)
    whole = jnp.concatenate([low, high], axis=1).transpose(0, 2, 1, 3).reshape(rank, cols)
    return new_left_t, right * whole


def factor(mesh):
    n_row, n_col = mesh.shape["row"], mesh.shape["col"]
    n_far, n_near = (3, 4) if n_row % 24 == 0 else (1, 2)
    shape = (n_row // (2 * n_far * n_near), n_far, n_near, 2, n_col)
    return Mesh(mesh.devices.reshape(shape), ("y", "zh", "zl", "c", "x"))


def solution(mesh):
    row = ("y", "zh", "zl", "c")
    return jax.shard_map(
        local,
        mesh=factor(mesh),
        in_specs=(P(row, "x"), P(None, row), P(None, "x")),
        out_specs=(P(None, row), P(None, "x")),
        check_vma=False,
    )
```

```python
import functools

import jax
import jax.numpy as jnp
from jax import lax
from jax.experimental import pallas as pl
from jax.experimental.pallas import tpu as pltpu
from jax.sharding import Mesh, PartitionSpec as P

SUB, LANE = 8, 128
ROWS_OF = 2
AHEAD = 2
F32, BF16 = jnp.float32, jnp.bfloat16
NT = (((1,), (1,)), ((), ()))


def split(x):
    high = x.astype(BF16)
    return high, (x - high.astype(F32)).astype(BF16)


def dot(a, b):
    return jnp.dot(a, b, preferred_element_type=F32)


def stack_left(left):
    rank = left.shape[0]
    wide = jnp.concatenate([left] * 4, axis=0).T
    high = wide.astype(BF16).astype(F32)
    lane = lax.broadcasted_iota(jnp.int32, wide.shape, 1)
    return jnp.where(lane < 2 * rank, high, wide - high).astype(BF16)


def pack_column(column):
    bands = column.shape[0] // SUB
    lane = lax.broadcasted_iota(jnp.int32, (SUB, LANE), 1) // (LANE // bands)
    tile = jnp.zeros((SUB, LANE), F32)
    for b in range(bands):
        tile = jnp.where(lane == b, column[b * SUB : (b + 1) * SUB], tile)
    return tile


def unpack_column(tile, bands):
    lane = lax.broadcasted_iota(jnp.int32, (SUB, LANE), 1) // (LANE // bands)
    return [jnp.max(jnp.where(lane == b, tile, 0.0), axis=1, keepdims=True) for b in range(bands)]


def quotient_of(stacked, right, cells):
    high, low = split(right)
    product = dot(stacked, jnp.concatenate([high, low, high, low], axis=0))
    return high, low, split(cells.astype(F32) / product)


def left_kernel(matrix_hbm, left_hbm, right_hbm, out_ref, matrix_ref, left_ref, right_ref, both_ref, rest_ref, sems, left_sem):
    rank, rows = left_ref.shape
    cols = right_ref.shape[1]
    width, chunk = widths(cols)
    steps = cols // width

    def fetches(i):
        at = pl.ds(pl.multiple_of(i * width, width), width)
        return (
            pltpu.make_async_copy(right_hbm.at[:, at], right_ref.at[:, at], sems.at[0, i]),
            pltpu.make_async_copy(matrix_hbm.at[:, at], matrix_ref.at[:, at], sems.at[1, i]),
        )

    fetch_left = pltpu.make_async_copy(left_hbm, left_ref, left_sem)
    fetch_left.start()
    for i in range(min(AHEAD, steps)):
        for fetch in fetches(i):
            fetch.start()
    both_ref[...] = jnp.zeros_like(both_ref)
    rest_ref[...] = jnp.zeros_like(rest_ref)
    fetch_left.wait()
    stacked = stack_left(left_ref[...])

    def body(i, summed):
        @pl.when(i + AHEAD < steps)
        def _():
            for fetch in fetches(i + AHEAD):
                fetch.start()

        for fetch in fetches(i):
            fetch.wait()
        highs, lows, q_highs, q_lows = [], [], [], []
        for c in range(width // chunk):
            at = pl.ds(pl.multiple_of(i * width + c * chunk, chunk), chunk)
            right = right_ref[:, at]
            high, low, (q_high, q_low) = quotient_of(stacked, right, matrix_ref[:, at])
            highs.append(high)
            lows.append(low)
            q_highs.append(q_high)
            q_lows.append(q_low)
            summed += sum(right[:, s : s + LANE] for s in range(0, chunk, LANE))
        high = jnp.concatenate(highs, axis=1)
        low = jnp.concatenate(lows, axis=1)
        both_ref[...] += lax.dot_general(
            jnp.concatenate(q_highs, axis=1), jnp.concatenate([high, low], axis=0), NT, preferred_element_type=F32
        )
        rest_ref[...] += lax.dot_general(
            jnp.concatenate(q_lows, axis=1), high, NT, preferred_element_type=F32
        )
        return summed

    mass = lax.fori_loop(0, steps, body, jnp.zeros((rank, LANE), F32))
    both = both_ref[...].T
    total = both[:rank] + both[rank:] + rest_ref[...].T
    bands, strips = rank // SUB, rows // LANE
    packed = pack_column(jnp.sum(mass, axis=1, keepdims=True))
    for peer in range(out_ref.shape[0]):
        for b in range(bands):
            for s in range(strips):
                out_ref[peer, b * strips + s] = total[b * SUB : (b + 1) * SUB, s * LANE : (s + 1) * LANE]
        out_ref[peer, bands * strips] = packed


def right_kernel(first, half_ref, matrix_ref, left_ref, right_ref, *refs):
    rank, rows = left_ref.shape
    bands, strips = rank // SUB, rows // LANE
    if first:
        source_ref, out_ref, kept_ref, new_ref = refs
        got = sum(source_ref[peer] for peer in range(source_ref.shape[0]))
        masses = unpack_column(got[bands * strips], bands)
        for b in range(bands):
            for s in range(strips):
                at = (slice(b * SUB, (b + 1) * SUB), slice(s * LANE, (s + 1) * LANE))
                value = left_ref[at] * got[b * strips + s] / masses[b]
                new_ref[at] = value
                kept_ref[at] = value
        new = kept_ref[...]
    else:
        (out_ref,) = refs
        new = left_ref[...]
    stacked = stack_left(new)
    new_high, new_low = split(new)
    pair = jnp.concatenate([new_high, new_low], axis=0)

    half = right_ref.shape[1] // 2
    width, chunk = widths(half)
    per_band = half // LANE
    wide = chunk // LANE
    sums = jnp.sum(new, axis=1, keepdims=True)
    for b in range(bands):
        out_ref[bands * per_band + b] = jnp.broadcast_to(sums[b * SUB : (b + 1) * SUB], (SUB, LANE))
    start = half_ref[0] * half

    def body(i, carry):
        for c in range(width // chunk):
            at = pl.ds(pl.multiple_of(start + i * width + c * chunk, chunk), chunk)
            _, _, (q_high, q_low) = quotient_of(stacked, right_ref[:, at], matrix_ref[:, at])
            both = dot(pair, q_high)
            total = both[:rank] + both[rank:] + dot(new_high, q_low)
            for b in range(bands):
                for s in range(wide):
                    out_ref[b * per_band + i * (width // LANE) + c * wide + s] = total[
                        b * SUB : (b + 1) * SUB, s * LANE : (s + 1) * LANE
                    ]
        return carry

    lax.fori_loop(0, half // width, body, 0)


def message_kernel(here_ref, there_ref, out_ref):
    peers, pairs = out_ref.shape[0], out_ref.shape[1] - 1
    per_tile = SUB // ROWS_OF
    each = pairs // per_tile
    half = peers * each
    bands = here_ref.shape[0] - half
    group = lax.broadcasted_iota(jnp.int32, (ROWS_OF, LANE), 1) // (LANE // per_tile)
    for b in range(bands):
        mass = here_ref[half + b] + there_ref[half + b]
        packed = jnp.zeros((ROWS_OF, LANE), F32)
        for r in range(per_tile):
            packed = jnp.where(group == r, mass[r * ROWS_OF : (r + 1) * ROWS_OF], packed)
        for p in range(b * peers // bands, (b + 1) * peers // bands):
            out_ref[p, pairs] = packed
    for t in range(half):
        tile = here_ref[t] + there_ref[t]
        for r in range(per_tile):
            out_ref[t // each, t % each * per_tile + r] = tile[r * ROWS_OF : (r + 1) * ROWS_OF]


def finish_kernel(part_ref, out_ref):
    per_tile = SUB // ROWS_OF
    pairs = part_ref.shape[1] - 1
    group = lax.broadcasted_iota(jnp.int32, (ROWS_OF, LANE), 1) // (LANE // per_tile)
    rows = [sum(part_ref[f, i] for f in range(part_ref.shape[0])) for i in range(pairs + 1)]
    mass = jnp.concatenate(
        [jnp.max(jnp.where(group == r, rows[pairs], 0.0), axis=1, keepdims=True) for r in range(per_tile)], axis=0
    )
    for e in range(out_ref.shape[1]):
        tile = jnp.concatenate(rows[e * per_tile : (e + 1) * per_tile], axis=0) / mass
        for p in range(out_ref.shape[0]):
            out_ref[p, e] = tile


def on_chip(kernel, name, shape, *args):
    return pl.pallas_call(
        kernel,
        name=name,
        out_shape=jax.ShapeDtypeStruct(shape, F32),
        in_specs=[ON_CHIP] * len(args),
        out_specs=ON_CHIP,
        compiler_params=PARAMS,
    )(*args)


def widths(cols):
    width = 1024 if cols % 1024 == 0 else LANE
    return width, min(width, 256)


def cost(rows, cols, rank):
    return pl.CostEstimate(
        flops=14 * rows * cols * rank, bytes_accessed=2 * rows * cols + 8 * rank * cols, transcendentals=rows * cols
    )


LEFT_LIMIT = 32 << 20
ON_CHIP = pl.BlockSpec(memory_space=pltpu.VMEM)
PARAMS = pltpu.CompilerParams(vmem_limit_bytes=32 << 20)


def left_phase(matrix, left_t, right, n_col):
    (rank, rows), cols = left_t.shape, right.shape[1]
    steps = cols // widths(cols)[0]
    n_tiles = rank * rows // (SUB * LANE) + 1
    return pl.pallas_call(
        left_kernel,
        name="left_phase",
        out_shape=[
            jax.ShapeDtypeStruct((n_col, n_tiles, SUB, LANE), F32),
            jax.ShapeDtypeStruct(matrix.shape, matrix.dtype),
            jax.ShapeDtypeStruct(left_t.shape, F32),
            jax.ShapeDtypeStruct(right.shape, F32),
        ],
        in_specs=[pl.BlockSpec(memory_space=pltpu.HBM)] * 3,
        out_specs=[ON_CHIP] * 4,
        scratch_shapes=[
            pltpu.VMEM((rows, 2 * rank), F32),
            pltpu.VMEM((rows, rank), F32),
            pltpu.SemaphoreType.DMA((2, steps)),
            pltpu.SemaphoreType.DMA,
        ],
        compiler_params=pltpu.CompilerParams(vmem_limit_bytes=LEFT_LIMIT),
        cost_estimate=cost(rows, cols, rank),
    )(*(pltpu.with_memory_space_constraint(a, pltpu.HBM) for a in (matrix, left_t, right)))


def right_phase(half, matrix, left_t, right, *source):
    (rank, rows), cols = left_t.shape, right.shape[1] // 2
    n_tiles = rank * cols // (SUB * LANE) + rank // SUB
    out_shape = [jax.ShapeDtypeStruct((n_tiles, SUB, LANE), F32)]
    if source:
        out_shape += [jax.ShapeDtypeStruct((rank, rows), F32)] * 2
    return pl.pallas_call(
        functools.partial(right_kernel, bool(source)),
        name="right_first" if source else "right_second",
        out_shape=out_shape,
        in_specs=[pl.BlockSpec(memory_space=pltpu.SMEM)] + [ON_CHIP] * (3 + len(source)),
        out_specs=[ON_CHIP] * len(out_shape),
        compiler_params=PARAMS,
        cost_estimate=cost(rows, cols, rank),
    )(half, matrix, left_t, right, *source)


def local(matrix, left_t, right):
    rank, cols = right.shape
    n_col, n_group = lax.axis_size("x"), lax.axis_size(("y", "zl"))
    n_far = lax.axis_size("zh")
    core = lax.axis_index("c")
    partner = [(0, 1), (1, 0)]
    own = jnp.reshape(core, (1,)).astype(jnp.int32)
    other = 1 - own
    left_t, own, other = lax.optimization_barrier((left_t, own, other))

    sent, matrix, left_t, right = left_phase(matrix, left_t, right, n_col)
    got = lax.all_to_all(sent, "x", 0, 0)
    for_partner, kept, new_left_t = right_phase(other, matrix, left_t, right, got)
    there = lax.ppermute(for_partner, "c", partner)
    (here,) = right_phase(own, matrix, kept, right)

    bands, strips = rank // SUB, cols // (2 * LANE)
    half = bands * strips
    each = half // n_group
    pairs = each * (SUB // ROWS_OF)
    message = on_chip(message_kernel, "message", (n_group, pairs + 1, ROWS_OF, LANE), here, there)
    part = jnp.sum(lax.all_to_all(message, ("y", "zl"), 0, 0), axis=0)
    part = lax.all_to_all(jnp.broadcast_to(part[None], (n_far, *part.shape)), "zh", 0, 0)
    done = on_chip(finish_kernel, "finish", (n_group, each, SUB, LANE), part)
    mine = lax.all_to_all(done, ("y", "zl"), 0, 0).reshape(bands, strips, SUB, LANE)
    theirs = lax.ppermute(mine, "c", partner)
    is_first = own[0] == 0
    low = jnp.where(is_first, mine, theirs)
    high = jnp.where(is_first, theirs, mine)
    whole = jnp.concatenate([low, high], axis=1).transpose(0, 2, 1, 3).reshape(rank, cols)
    return new_left_t, right * whole


def factor(mesh):
    n_row, n_col = mesh.shape["row"], mesh.shape["col"]
    n_far, n_near = (6, 2) if n_row % 24 == 0 else (1, 2)
    shape = (n_row // (2 * n_far * n_near), n_far, n_near, 2, n_col)
    return Mesh(mesh.devices.reshape(shape), ("y", "zh", "zl", "c", "x"))


def solution(mesh):
    row = ("y", "zh", "zl", "c")
    return jax.shard_map(
        local,
        mesh=factor(mesh),
        in_specs=(P(row, "x"), P(None, row), P(None, "x")),
        out_specs=(P(None, row), P(None, "x")),
        check_vma=False,
    )
```

```python
import functools

import jax
import jax.numpy as jnp
from jax import lax
from jax.experimental import pallas as pl
from jax.experimental.pallas import tpu as pltpu
from jax.sharding import Mesh, PartitionSpec as P

SUB, LANE = 8, 128
ROWS_OF = 2
LEFT_STEP, RIGHT_STEP = 2048, 3072
F32, BF16 = jnp.float32, jnp.bfloat16
NT = (((1,), (1,)), ((), ()))


def split(x):
    high = x.astype(BF16)
    return high, (x - high.astype(F32)).astype(BF16)


def dot(a, b):
    return jnp.dot(a, b, preferred_element_type=F32)


def stack_left(left):
    rank = left.shape[0]
    wide = jnp.concatenate([left] * 4, axis=0).T
    high = wide.astype(BF16).astype(F32)
    lane = lax.broadcasted_iota(jnp.int32, wide.shape, 1)
    return jnp.where(lane < 2 * rank, high, wide - high).astype(BF16)


def pack_column(column):
    bands = column.shape[0] // SUB
    lane = lax.broadcasted_iota(jnp.int32, (SUB, LANE), 1) // (LANE // bands)
    tile = jnp.zeros((SUB, LANE), F32)
    for b in range(bands):
        tile = jnp.where(lane == b, column[b * SUB : (b + 1) * SUB], tile)
    return tile


def unpack_column(tile, bands):
    lane = lax.broadcasted_iota(jnp.int32, (SUB, LANE), 1) // (LANE // bands)
    return [jnp.max(jnp.where(lane == b, tile, 0.0), axis=1, keepdims=True) for b in range(bands)]


def quotient_of(stacked, right, cells):
    high, low = split(right)
    product = dot(stacked, jnp.concatenate([high, low, high, low], axis=0))
    return high, low, split(cells.astype(F32) / product)


def left_kernel(matrix_hbm, left_hbm, right_hbm, out_ref, matrix_ref, left_ref, right_ref, both_ref, rest_ref, sems, left_sem):
    rank, rows = left_ref.shape
    cols = right_ref.shape[1]
    width, chunk = widths(cols, LEFT_STEP)
    steps, piece = cols // width, width // 2

    def fetches(i):
        at = pl.ds(pl.multiple_of(i * piece, piece), piece)
        return (
            pltpu.make_async_copy(right_hbm.at[:, at], right_ref.at[:, at], sems.at[0, i]),
            pltpu.make_async_copy(matrix_hbm.at[:, at], matrix_ref.at[:, at], sems.at[1, i]),
        )

    fetch_left = pltpu.make_async_copy(left_hbm, left_ref, left_sem)
    fetch_left.start()
    for i in range(2 if steps == 1 else 3):
        for fetch in fetches(i):
            fetch.start()
    both_ref[...] = jnp.zeros_like(both_ref)
    rest_ref[...] = jnp.zeros_like(rest_ref)
    fetch_left.wait()
    stacked = stack_left(left_ref[...])

    def body(i, summed):
        for ahead in (3, 4):
            @pl.when(2 * i + ahead < 2 * steps)
            def _():
                for fetch in fetches(2 * i + ahead):
                    fetch.start()

        highs, lows, q_highs, q_lows = [], [], [], []
        for c in range(width // chunk):
            if c * chunk % piece == 0:
                for fetch in fetches(2 * i + c * chunk // piece):
                    fetch.wait()
            at = pl.ds(pl.multiple_of(i * width + c * chunk, chunk), chunk)
            right = right_ref[:, at]
            high, low, (q_high, q_low) = quotient_of(stacked, right, matrix_ref[:, at])
            highs.append(high)
            lows.append(low)
            q_highs.append(q_high)
            q_lows.append(q_low)
            summed += sum(right[:, s : s + LANE] for s in range(0, chunk, LANE))
        high = jnp.concatenate(highs, axis=1)
        low = jnp.concatenate(lows, axis=1)
        both_ref[...] += lax.dot_general(
            jnp.concatenate([high, low], axis=0), jnp.concatenate(q_highs, axis=1), NT, preferred_element_type=F32
        )
        rest_ref[...] += lax.dot_general(
            high, jnp.concatenate(q_lows, axis=1), NT, preferred_element_type=F32
        )
        return summed

    mass = lax.fori_loop(0, steps, body, jnp.zeros((rank, LANE), F32))
    total = both_ref[:rank] + both_ref[rank:] + rest_ref[...]
    bands, strips = rank // SUB, rows // LANE
    packed = pack_column(jnp.sum(mass, axis=1, keepdims=True))
    for peer in range(out_ref.shape[0]):
        for b in range(bands):
            for s in range(strips):
                out_ref[peer, b * strips + s] = total[b * SUB : (b + 1) * SUB, s * LANE : (s + 1) * LANE]
        out_ref[peer, bands * strips] = packed


def right_kernel(first, half_ref, matrix_ref, left_ref, right_ref, *refs):
    rank, rows = left_ref.shape
    bands, strips = rank // SUB, rows // LANE
    if first:
        source_ref, out_ref, kept_ref, new_ref = refs
        got = sum(source_ref[peer] for peer in range(source_ref.shape[0]))
        masses = unpack_column(got[bands * strips], bands)
        for b in range(bands):
            for s in range(strips):
                at = (slice(b * SUB, (b + 1) * SUB), slice(s * LANE, (s + 1) * LANE))
                value = left_ref[at] * got[b * strips + s] / masses[b]
                new_ref[at] = value
                kept_ref[at] = value
        new = kept_ref[...]
    else:
        (out_ref,) = refs
        new = left_ref[...]
    stacked = stack_left(new)
    new_high, new_low = split(new)
    pair = jnp.concatenate([new_high, new_low], axis=0)

    half = right_ref.shape[1] // 2
    width, chunk = widths(half, RIGHT_STEP)
    per_band = half // LANE
    wide = chunk // LANE
    sums = jnp.sum(new, axis=1, keepdims=True)
    for b in range(bands):
        out_ref[bands * per_band + b] = jnp.broadcast_to(sums[b * SUB : (b + 1) * SUB], (SUB, LANE))
    start = half_ref[0] * half

    def body(i, carry):
        for c in range(width // chunk):
            at = pl.ds(pl.multiple_of(start + i * width + c * chunk, chunk), chunk)
            _, _, (q_high, q_low) = quotient_of(stacked, right_ref[:, at], matrix_ref[:, at])
            both = dot(pair, q_high)
            total = both[:rank] + both[rank:] + dot(new_high, q_low)
            for b in range(bands):
                for s in range(wide):
                    out_ref[b * per_band + i * (width // LANE) + c * wide + s] = total[
                        b * SUB : (b + 1) * SUB, s * LANE : (s + 1) * LANE
                    ]
        return carry

    lax.fori_loop(0, half // width, body, 0)


def message_kernel(here_ref, there_ref, out_ref):
    peers, pairs = out_ref.shape[0], out_ref.shape[1] - 1
    per_tile = SUB // ROWS_OF
    each = pairs // per_tile
    half = peers * each
    bands = here_ref.shape[0] - half
    group = lax.broadcasted_iota(jnp.int32, (ROWS_OF, LANE), 1) // (LANE // per_tile)
    for b in range(bands):
        mass = here_ref[half + b] + there_ref[half + b]
        packed = jnp.zeros((ROWS_OF, LANE), F32)
        for r in range(per_tile):
            packed = jnp.where(group == r, mass[r * ROWS_OF : (r + 1) * ROWS_OF], packed)
        for p in range(b * peers // bands, (b + 1) * peers // bands):
            out_ref[p, pairs] = packed
    for t in range(half):
        tile = here_ref[t] + there_ref[t]
        for r in range(per_tile):
            out_ref[t // each, t % each * per_tile + r] = tile[r * ROWS_OF : (r + 1) * ROWS_OF]


def finish_kernel(part_ref, out_ref):
    per_tile = SUB // ROWS_OF
    pairs = part_ref.shape[1] - 1
    group = lax.broadcasted_iota(jnp.int32, (ROWS_OF, LANE), 1) // (LANE // per_tile)
    rows = [sum(part_ref[f, i] for f in range(part_ref.shape[0])) for i in range(pairs + 1)]
    mass = jnp.concatenate(
        [jnp.max(jnp.where(group == r, rows[pairs], 0.0), axis=1, keepdims=True) for r in range(per_tile)], axis=0
    )
    for e in range(out_ref.shape[1]):
        tile = jnp.concatenate(rows[e * per_tile : (e + 1) * per_tile], axis=0) / mass
        for p in range(out_ref.shape[0]):
            out_ref[p, e] = tile


def on_chip(kernel, name, shape, *args):
    return pl.pallas_call(
        kernel,
        name=name,
        out_shape=jax.ShapeDtypeStruct(shape, F32),
        in_specs=[ON_CHIP] * len(args),
        out_specs=ON_CHIP,
        compiler_params=PARAMS,
    )(*args)


def widths(cols, most):
    width = next((w for w in (3072, 2048, 1024) if w <= most and cols % w == 0), LANE)
    return width, min(width, 256)


def cost(rows, cols, rank):
    return pl.CostEstimate(
        flops=14 * rows * cols * rank, bytes_accessed=2 * rows * cols + 8 * rank * cols, transcendentals=rows * cols
    )


LEFT_LIMIT = 32 << 20
ON_CHIP = pl.BlockSpec(memory_space=pltpu.VMEM)
PARAMS = pltpu.CompilerParams(vmem_limit_bytes=32 << 20)


def left_phase(matrix, left_t, right, n_col):
    (rank, rows), cols = left_t.shape, right.shape[1]
    steps = 2 * (cols // widths(cols, LEFT_STEP)[0])
    n_tiles = rank * rows // (SUB * LANE) + 1
    return pl.pallas_call(
        left_kernel,
        name="left_phase",
        out_shape=[
            jax.ShapeDtypeStruct((n_col, n_tiles, SUB, LANE), F32),
            jax.ShapeDtypeStruct(matrix.shape, matrix.dtype),
            jax.ShapeDtypeStruct(left_t.shape, F32),
            jax.ShapeDtypeStruct(right.shape, F32),
        ],
        in_specs=[pl.BlockSpec(memory_space=pltpu.HBM)] * 3,
        out_specs=[ON_CHIP] * 4,
        scratch_shapes=[
            pltpu.VMEM((2 * rank, rows), F32),
            pltpu.VMEM((rank, rows), F32),
            pltpu.SemaphoreType.DMA((2, steps)),
            pltpu.SemaphoreType.DMA,
        ],
        compiler_params=pltpu.CompilerParams(vmem_limit_bytes=LEFT_LIMIT),
        cost_estimate=cost(rows, cols, rank),
    )(*(pltpu.with_memory_space_constraint(a, pltpu.HBM) for a in (matrix, left_t, right)))


def right_phase(half, matrix, left_t, right, *source):
    (rank, rows), cols = left_t.shape, right.shape[1] // 2
    n_tiles = rank * cols // (SUB * LANE) + rank // SUB
    out_shape = [jax.ShapeDtypeStruct((n_tiles, SUB, LANE), F32)]
    if source:
        out_shape += [jax.ShapeDtypeStruct((rank, rows), F32)] * 2
    return pl.pallas_call(
        functools.partial(right_kernel, bool(source)),
        name="right_first" if source else "right_second",
        out_shape=out_shape,
        in_specs=[pl.BlockSpec(memory_space=pltpu.SMEM)] + [ON_CHIP] * (3 + len(source)),
        out_specs=[ON_CHIP] * len(out_shape),
        compiler_params=PARAMS,
        cost_estimate=cost(rows, cols, rank),
    )(half, matrix, left_t, right, *source)


def local(matrix, left_t, right):
    rank, cols = right.shape
    n_col, n_group = lax.axis_size("x"), lax.axis_size(("y", "zl"))
    n_far = lax.axis_size("zh")
    core = lax.axis_index("c")
    partner = [(0, 1), (1, 0)]
    own = jnp.reshape(core, (1,)).astype(jnp.int32)
    other = 1 - own
    left_t, own, other = lax.optimization_barrier((left_t, own, other))

    sent, matrix, left_t, right = left_phase(matrix, left_t, right, n_col)
    got = lax.all_to_all(sent, "x", 0, 0)
    for_partner, kept, new_left_t = right_phase(other, matrix, left_t, right, got)
    there = lax.ppermute(for_partner, "c", partner)
    (here,) = right_phase(own, matrix, kept, right)

    bands, strips = rank // SUB, cols // (2 * LANE)
    half = bands * strips
    each = half // n_group
    pairs = each * (SUB // ROWS_OF)
    message = on_chip(message_kernel, "message", (n_group, pairs + 1, ROWS_OF, LANE), here, there)
    part = jnp.sum(lax.all_to_all(message, ("y", "zl"), 0, 0), axis=0)
    part = lax.all_to_all(jnp.broadcast_to(part[None], (n_far, *part.shape)), "zh", 0, 0)
    done = on_chip(finish_kernel, "finish", (n_group, each, SUB, LANE), part)
    mine = lax.all_to_all(done, ("y", "zl"), 0, 0).reshape(bands, strips, SUB, LANE)
    theirs = lax.ppermute(mine, "c", partner)
    is_first = own[0] == 0
    low = jnp.where(is_first, mine, theirs)
    high = jnp.where(is_first, theirs, mine)
    whole = jnp.concatenate([low, high], axis=1).transpose(0, 2, 1, 3).reshape(rank, cols)
    return new_left_t, right * whole


def factor(mesh):
    n_row, n_col = mesh.shape["row"], mesh.shape["col"]
    n_far, n_near = (6, 2) if n_row % 24 == 0 else (1, 2)
    shape = (n_row // (2 * n_far * n_near), n_far, n_near, 2, n_col)
    return Mesh(mesh.devices.reshape(shape), ("y", "zh", "zl", "c", "x"))


def solution(mesh):
    row = ("y", "zh", "zl", "c")
    return jax.shard_map(
        local,
        mesh=factor(mesh),
        in_specs=(P(row, "x"), P(None, row), P(None, "x")),
        out_specs=(P(None, row), P(None, "x")),
        check_vma=False,
    )
```

```python
import functools

import jax
import jax.numpy as jnp
from jax import lax
from jax.experimental import pallas as pl
from jax.experimental.pallas import tpu as pltpu
from jax.sharding import Mesh, PartitionSpec as P

SUB, LANE = 8, 128
ROWS_OF = 2
LEFT_STEP, RIGHT_STEP = 3072, 3072
F32, BF16 = jnp.float32, jnp.bfloat16
NT = (((1,), (1,)), ((), ()))


def split(x):
    high = x.astype(BF16)
    return high, (x - high.astype(F32)).astype(BF16)


def dot(a, b):
    return jnp.dot(a, b, preferred_element_type=F32)


def stack_left(left):
    rank = left.shape[0]
    wide = jnp.concatenate([left] * 4, axis=0).T
    high = wide.astype(BF16).astype(F32)
    lane = lax.broadcasted_iota(jnp.int32, wide.shape, 1)
    return jnp.where(lane < 2 * rank, high, wide - high).astype(BF16)


def pack_column(column):
    bands = column.shape[0] // SUB
    lane = lax.broadcasted_iota(jnp.int32, (SUB, LANE), 1) // (LANE // bands)
    tile = jnp.zeros((SUB, LANE), F32)
    for b in range(bands):
        tile = jnp.where(lane == b, column[b * SUB : (b + 1) * SUB], tile)
    return tile


def unpack_column(tile, bands):
    lane = lax.broadcasted_iota(jnp.int32, (SUB, LANE), 1) // (LANE // bands)
    return [jnp.max(jnp.where(lane == b, tile, 0.0), axis=1, keepdims=True) for b in range(bands)]


def quotient_of(stacked, right, cells):
    high, low = split(right)
    product = dot(stacked, jnp.concatenate([high, low, high, low], axis=0))
    return high, low, split(cells.astype(F32) / product)


def left_kernel(matrix_hbm, left_hbm, right_hbm, out_ref, matrix_ref, left_ref, right_ref, both_ref, rest_ref, sems, left_sem):
    rank, rows = left_ref.shape
    cols = right_ref.shape[1]
    width, chunk = widths(cols, LEFT_STEP)
    steps, piece = cols // width, width // 2

    def fetches(i):
        at = pl.ds(pl.multiple_of(i * piece, piece), piece)
        return (
            pltpu.make_async_copy(right_hbm.at[:, at], right_ref.at[:, at], sems.at[0, i]),
            pltpu.make_async_copy(matrix_hbm.at[:, at], matrix_ref.at[:, at], sems.at[1, i]),
        )

    fetch_left = pltpu.make_async_copy(left_hbm, left_ref, left_sem)
    fetch_left.start()
    for i in range(2 if steps == 1 else 3):
        for fetch in fetches(i):
            fetch.start()
    both_ref[...] = jnp.zeros_like(both_ref)
    rest_ref[...] = jnp.zeros_like(rest_ref)
    fetch_left.wait()
    stacked = stack_left(left_ref[...])

    def body(i, summed):
        for ahead in (3, 4):
            @pl.when(2 * i + ahead < 2 * steps)
            def _():
                for fetch in fetches(2 * i + ahead):
                    fetch.start()

        highs, lows, q_highs, q_lows = [], [], [], []
        for c in range(width // chunk):
            if c * chunk % piece == 0:
                for fetch in fetches(2 * i + c * chunk // piece):
                    fetch.wait()
            at = pl.ds(pl.multiple_of(i * width + c * chunk, chunk), chunk)
            right = right_ref[:, at]
            high, low, (q_high, q_low) = quotient_of(stacked, right, matrix_ref[:, at])
            highs.append(high)
            lows.append(low)
            q_highs.append(q_high)
            q_lows.append(q_low)
            summed += sum(right[:, s : s + LANE] for s in range(0, chunk, LANE))
        high = jnp.concatenate(highs, axis=1)
        low = jnp.concatenate(lows, axis=1)
        both_ref[...] += lax.dot_general(
            jnp.concatenate(q_highs, axis=1), jnp.concatenate([high, low], axis=0), NT, preferred_element_type=F32
        )
        rest_ref[...] += lax.dot_general(
            jnp.concatenate(q_lows, axis=1), high, NT, preferred_element_type=F32
        )
        return summed

    mass = lax.fori_loop(0, steps, body, jnp.zeros((rank, LANE), F32))
    both = both_ref[...].T
    total = both[:rank] + both[rank:] + rest_ref[...].T
    bands, strips = rank // SUB, rows // LANE
    packed = pack_column(jnp.sum(mass, axis=1, keepdims=True))
    for peer in range(out_ref.shape[0]):
        for b in range(bands):
            for s in range(strips):
                out_ref[peer, b * strips + s] = total[b * SUB : (b + 1) * SUB, s * LANE : (s + 1) * LANE]
        out_ref[peer, bands * strips] = packed


def right_kernel(first, half_ref, matrix_ref, left_ref, right_ref, *refs):
    rank, rows = left_ref.shape
    bands, strips = rank // SUB, rows // LANE
    if first:
        source_ref, out_ref, kept_ref, new_ref = refs
        got = sum(source_ref[peer] for peer in range(source_ref.shape[0]))
        masses = unpack_column(got[bands * strips], bands)
        for b in range(bands):
            for s in range(strips):
                at = (slice(b * SUB, (b + 1) * SUB), slice(s * LANE, (s + 1) * LANE))
                value = left_ref[at] * got[b * strips + s] / masses[b]
                new_ref[at] = value
                kept_ref[at] = value
        new = kept_ref[...]
    else:
        (out_ref,) = refs
        new = left_ref[...]
    stacked = stack_left(new)
    new_high, new_low = split(new)
    pair = jnp.concatenate([new_high, new_low], axis=0)

    half = right_ref.shape[1] // 2
    width, chunk = widths(half, RIGHT_STEP)
    per_band = half // LANE
    wide = chunk // LANE
    sums = jnp.sum(new, axis=1, keepdims=True)
    for b in range(bands):
        out_ref[bands * per_band + b] = jnp.broadcast_to(sums[b * SUB : (b + 1) * SUB], (SUB, LANE))
    start = half_ref[0] * half

    def body(i, carry):
        for c in range(width // chunk):
            at = pl.ds(pl.multiple_of(start + i * width + c * chunk, chunk), chunk)
            _, _, (q_high, q_low) = quotient_of(stacked, right_ref[:, at], matrix_ref[:, at])
            both = dot(pair, q_high)
            total = both[:rank] + both[rank:] + dot(new_high, q_low)
            for b in range(bands):
                for s in range(wide):
                    out_ref[b * per_band + i * (width // LANE) + c * wide + s] = total[
                        b * SUB : (b + 1) * SUB, s * LANE : (s + 1) * LANE
                    ]
        return carry

    lax.fori_loop(0, half // width, body, 0)


def message_kernel(here_ref, there_ref, out_ref):
    peers, pairs = out_ref.shape[0], out_ref.shape[1] - 1
    per_tile = SUB // ROWS_OF
    each = pairs // per_tile
    half = peers * each
    bands = here_ref.shape[0] - half
    group = lax.broadcasted_iota(jnp.int32, (ROWS_OF, LANE), 1) // (LANE // per_tile)
    for b in range(bands):
        mass = here_ref[half + b] + there_ref[half + b]
        packed = jnp.zeros((ROWS_OF, LANE), F32)
        for r in range(per_tile):
            packed = jnp.where(group == r, mass[r * ROWS_OF : (r + 1) * ROWS_OF], packed)
        for p in range(b * peers // bands, (b + 1) * peers // bands):
            out_ref[p, pairs] = packed
    for t in range(half):
        tile = here_ref[t] + there_ref[t]
        for r in range(per_tile):
            out_ref[t // each, t % each * per_tile + r] = tile[r * ROWS_OF : (r + 1) * ROWS_OF]


def finish_kernel(part_ref, out_ref):
    per_tile = SUB // ROWS_OF
    pairs = part_ref.shape[1] - 1
    group = lax.broadcasted_iota(jnp.int32, (ROWS_OF, LANE), 1) // (LANE // per_tile)
    rows = [sum(part_ref[f, i] for f in range(part_ref.shape[0])) for i in range(pairs + 1)]
    mass = jnp.concatenate(
        [jnp.max(jnp.where(group == r, rows[pairs], 0.0), axis=1, keepdims=True) for r in range(per_tile)], axis=0
    )
    for e in range(out_ref.shape[1]):
        tile = jnp.concatenate(rows[e * per_tile : (e + 1) * per_tile], axis=0) / mass
        for p in range(out_ref.shape[0]):
            out_ref[p, e] = tile


def on_chip(kernel, name, shape, *args):
    return pl.pallas_call(
        kernel,
        name=name,
        out_shape=jax.ShapeDtypeStruct(shape, F32),
        in_specs=[ON_CHIP] * len(args),
        out_specs=ON_CHIP,
        compiler_params=PARAMS,
    )(*args)


def widths(cols, most):
    width = next((w for w in (3072, 2048, 1024) if w <= most and cols % w == 0), LANE)
    return width, min(width, 256)


def cost(rows, cols, rank):
    return pl.CostEstimate(
        flops=14 * rows * cols * rank, bytes_accessed=2 * rows * cols + 8 * rank * cols, transcendentals=rows * cols
    )


LEFT_LIMIT = 32 << 20
ON_CHIP = pl.BlockSpec(memory_space=pltpu.VMEM)
PARAMS = pltpu.CompilerParams(vmem_limit_bytes=32 << 20)


def left_phase(matrix, left_t, right, n_col):
    (rank, rows), cols = left_t.shape, right.shape[1]
    steps = 2 * (cols // widths(cols, LEFT_STEP)[0])
    n_tiles = rank * rows // (SUB * LANE) + 1
    return pl.pallas_call(
        left_kernel,
        name="left_phase",
        out_shape=[
            jax.ShapeDtypeStruct((n_col, n_tiles, SUB, LANE), F32),
            jax.ShapeDtypeStruct(matrix.shape, matrix.dtype),
            jax.ShapeDtypeStruct(left_t.shape, F32),
            jax.ShapeDtypeStruct(right.shape, F32),
        ],
        in_specs=[pl.BlockSpec(memory_space=pltpu.HBM)] * 3,
        out_specs=[ON_CHIP] * 4,
        scratch_shapes=[
            pltpu.VMEM((rows, 2 * rank), F32),
            pltpu.VMEM((rows, rank), F32),
            pltpu.SemaphoreType.DMA((2, steps)),
            pltpu.SemaphoreType.DMA,
        ],
        compiler_params=pltpu.CompilerParams(vmem_limit_bytes=LEFT_LIMIT),
        cost_estimate=cost(rows, cols, rank),
    )(*(pltpu.with_memory_space_constraint(a, pltpu.HBM) for a in (matrix, left_t, right)))


def right_phase(half, matrix, left_t, right, *source):
    (rank, rows), cols = left_t.shape, right.shape[1] // 2
    n_tiles = rank * cols // (SUB * LANE) + rank // SUB
    out_shape = [jax.ShapeDtypeStruct((n_tiles, SUB, LANE), F32)]
    if source:
        out_shape += [jax.ShapeDtypeStruct((rank, rows), F32)] * 2
    return pl.pallas_call(
        functools.partial(right_kernel, bool(source)),
        name="right_first" if source else "right_second",
        out_shape=out_shape,
        in_specs=[pl.BlockSpec(memory_space=pltpu.SMEM)] + [ON_CHIP] * (3 + len(source)),
        out_specs=[ON_CHIP] * len(out_shape),
        compiler_params=PARAMS,
        cost_estimate=cost(rows, cols, rank),
    )(half, matrix, left_t, right, *source)


def local(matrix, left_t, right):
    rank, cols = right.shape
    n_col, n_group = lax.axis_size("x"), lax.axis_size(("y", "zl"))
    n_far = lax.axis_size("zh")
    core = lax.axis_index("c")
    partner = [(0, 1), (1, 0)]
    own = jnp.reshape(core, (1,)).astype(jnp.int32)
    other = 1 - own
    left_t, own, other = lax.optimization_barrier((left_t, own, other))

    sent, matrix, left_t, right = left_phase(matrix, left_t, right, n_col)
    got = lax.all_to_all(sent, "x", 0, 0)
    for_partner, kept, new_left_t = right_phase(other, matrix, left_t, right, got)
    there = lax.ppermute(for_partner, "c", partner)
    (here,) = right_phase(own, matrix, kept, right)

    bands, strips = rank // SUB, cols // (2 * LANE)
    half = bands * strips
    each = half // n_group
    pairs = each * (SUB // ROWS_OF)
    message = on_chip(message_kernel, "message", (n_group, pairs + 1, ROWS_OF, LANE), here, there)
    part = jnp.sum(lax.all_to_all(message, ("y", "zl"), 0, 0), axis=0)
    part = lax.all_to_all(jnp.broadcast_to(part[None], (n_far, *part.shape)), "zh", 0, 0)
    done = on_chip(finish_kernel, "finish", (n_group, each, SUB, LANE), part)
    mine = lax.all_to_all(done, ("y", "zl"), 0, 0).reshape(bands, strips, SUB, LANE)
    theirs = lax.ppermute(mine, "c", partner)
    is_first = own[0] == 0
    low = jnp.where(is_first, mine, theirs)
    high = jnp.where(is_first, theirs, mine)
    whole = jnp.concatenate([low, high], axis=1).transpose(0, 2, 1, 3).reshape(rank, cols)
    return new_left_t, right * whole


def factor(mesh):
    n_row, n_col = mesh.shape["row"], mesh.shape["col"]
    n_far, n_near = (6, 2) if n_row % 24 == 0 else (1, 2)
    shape = (n_row // (2 * n_far * n_near), n_far, n_near, 2, n_col)
    return Mesh(mesh.devices.reshape(shape), ("y", "zh", "zl", "c", "x"))


def solution(mesh):
    row = ("y", "zh", "zl", "c")
    return jax.shard_map(
        local,
        mesh=factor(mesh),
        in_specs=(P(row, "x"), P(None, row), P(None, "x")),
        out_specs=(P(None, row), P(None, "x")),
        check_vma=False,
    )
```
